256 devices in a mesh: tile: 32 (over x, z_lo, core), mode: 8 (over z_hi, y).
Axes of the slice: x: 4, y: 4, z: 8 (z_hi: 2, z_lo: 4; z = z_hi * 4 + z_lo), core: 2. Of those that a mesh axis runs over, the one named last changes fastest.
Arguments:
- object_field: float32 [2, 8192, 1024], P(None, 'tile'), may hold values from -6 to 6
- probe_modes: float32 [2, 8, 256, 256], P(None, 'mode'), may hold values from -1.5 to 1.5
- measured: float32 [256, 256, 256], P('tile'), may hold values from 0.05 to 4
- row_starts: int32 [256], P('tile'), may hold values from -128 to 128, as said below
- col_starts: int32 [256], P('tile'), may hold values from 0 to 768
- live_counts: int32 [32], P('tile'), may hold values from 1 to 8, 192 in all
Outputs:
- object_grad: float32 [2, 8192, 1024], P(None, 'tile', 'mode')
- probe_grad: float32 [2, 8, 256, 256], P(None, 'mode')
The draws below stay inside these ranges and needn't reach their ends.
Inputs may be any that keep to these rules, and one draw needn't show every extreme that they name: A window lies inside the object: on tile 0 row_starts is at least 0, on the last tile at most 0; elsewhere a window reaches at most 128 rows into the tile above or below. `live_counts`: slots of a tile from its count on are unused.
All inputs are finite; a program needn't handle non-finite values. No bound on the sum of `live_counts` on one device may be relied on, other than what follows from the above.
Results may differ from the reference program's by a relative error of at most 0.0056.
Values sent between devices are 32-bit elements; how exact they have to be, the bound alone decides.
No kernel may reach another device: no remote copies, remote signals or barrier semaphores. Data moves between devices by JAX's collectives and lax.ppermute only.
A program may use at most 64 MiB of HBM per device.

```python
import math
import jax
import jax.numpy as jnp
import numpy as np
from jax import lax

WIN = 256
MODES = 8
POS_DEV = 8
TILE_R = 256
OBJ_C = 1024
HALF = 128
N_POS = 256
OBJ_R = 8192
N_TILE = 32


def draw_row_starts(key, part):
    mixed_key = jax.random.fold_in(key, 11)
    devices_count = N_POS // POS_DEV
    slot_index = jnp.arange(N_POS, dtype=jnp.int32)
    owner_tile = slot_index // POS_DEV
    within = slot_index % POS_DEV
    lowest = jnp.where(owner_tile == 0, 0, 0 - HALF)
    highest = jnp.where(owner_tile == devices_count - 1, TILE_R - WIN, TILE_R - HALF)
    random_bits = jax.random.randint(mixed_key, (N_POS,), 0, 1048576, dtype=jnp.int32)
    row_start = lowest + random_bits % (highest - lowest + 1)
    row_start = jnp.where((owner_tile == 1) & (within == 0), 0 - HALF, row_start)
    row_start = jnp.where((owner_tile == 1) & (within == 1), TILE_R - HALF, row_start)
    return row_start.astype(jnp.int32)


def draw_col_starts(key, part):
    mixed_key = jax.random.fold_in(key, 23)
    slot_index = jnp.arange(N_POS, dtype=jnp.int32)
    within = slot_index % POS_DEV
    random_bits = jax.random.randint(mixed_key, (N_POS,), 0, 1048576, dtype=jnp.int32)
    col_start = random_bits % (OBJ_C - WIN + 1)
    col_start = jnp.where(within == 0, 0, col_start)
    col_start = jnp.where(within == 1, OBJ_C - WIN, col_start)
    return col_start.astype(jnp.int32)


def level_of(rng, dims, pieces, low, top_value):
    loudness = 1.0
    for dim, blocks in pieces:
        draws = jax.random.uniform(jax.random.fold_in(jax.random.fold_in(rng, 6), dim), (blocks,), jnp.float32, low / len(pieces), top_value / len(pieces))
        loudness = loudness * jnp.repeat(jnp.exp(draws), dims[dim] // blocks).reshape((-1,) + (1,) * (len(dims) - 1 - dim))
    return loudness


def length_profile(number_of, total, reach, slope):
    portions = [(1 << 20) // math.isqrt(grade ** slope) + 1 for grade in range(2, number_of + 1)]
    spare, holding = total - reach - (number_of - 1), [1] * (number_of - 1)
    while spare > 0:
        candidates = [i for i in range(number_of - 1) if holding[i] < reach]
        mass, budget = sum([portions[i] for i in candidates]), spare
        for i in candidates:
            more = min(reach - holding[i], max(1, budget * portions[i] // mass), spare)
            holding[i] = holding[i] + more
            spare = spare - more
    return np.array([reach] + holding)


def uneven_parts(rng, number_of, total, limit, slope):
    if number_of == 2:
        one = jax.random.randint(rng, (), max(1, total - limit), min(limit, total - 1) + 1)
        return jnp.stack([one, total - one])
    sizes = jnp.asarray(length_profile(number_of, total, limit, slope), jnp.int32)
    couples = (number_of - 1) // 2
    giver, receiver = sizes[1:1 + 2 * couples:2], sizes[2:2 + 2 * couples:2]
    slack = jnp.minimum(giver - 1, limit - receiver)
    passed = jax.random.randint(jax.random.fold_in(rng, 1), (couples,), 0, 1 << 20) % (slack + 1)
    sizes = sizes.at[1:1 + 2 * couples:2].set(giver - passed).at[2:2 + 2 * couples:2].set(receiver + passed)
    return sizes[jax.random.permutation(jax.random.fold_in(rng, 2), number_of)]


def normal_values(key, shape, spread, limit, cuts=(), kind=jnp.bfloat16):
    drawn = jax.random.normal(key, shape, jnp.float32) * spread
    if len(cuts) > 0:
        drawn = level_of(key, shape, cuts, -0.22, 0.18) * drawn
    return jnp.clip(drawn, min=-limit, max=limit).astype(kind)


def setup_inputs(seed: int = 0) -> dict:
    arg_keys = jax.random.split(jax.random.key(seed), 7)
    object_field = normal_values(arg_keys[0], (2, OBJ_R, OBJ_C), 0.7, 6.0, ((1, 32),), jnp.float32)
    probe_modes = normal_values(arg_keys[1], (2, MODES, WIN, WIN), (2 * MODES) ** -0.5, 1.5, ((1, 8),), jnp.float32)
    measured = jnp.clip(jnp.exp(math.log(4.0) - 4.3820266 * jax.random.uniform(arg_keys[2], (N_POS, WIN, WIN), jnp.float32) ** level_of(arg_keys[2], (N_POS, WIN, WIN), ((0, 32),), -0.2, 0.2)), 0.05, 4.0)
    row_starts = draw_row_starts(jax.random.fold_in(arg_keys[6], 71), 0)
    col_starts = draw_col_starts(jax.random.fold_in(arg_keys[6], 71), 0)
    live_counts = uneven_parts(arg_keys[5], N_TILE, N_POS * 3 // 4, POS_DEV, 2).astype(jnp.int32)
    return dict(object_field=object_field, probe_modes=probe_modes, measured=measured, row_starts=row_starts, col_starts=col_starts, live_counts=live_counts)


def dft_blocks(window, conj_sign):
    index_range = jnp.arange(window, dtype=jnp.int32)
    phases = index_range[:, None] * index_range[None, :] % window
    angles = phases.astype(jnp.float32) * (-2.0 * math.pi / window)
    norm_scale = 1.0 / math.sqrt(window)
    cosine_table = (jnp.cos(angles) * norm_scale).astype(jnp.bfloat16)
    sine_table = (jnp.sin(angles) * (norm_scale * conj_sign)).astype(jnp.bfloat16)
    return jnp.stack([jnp.stack([cosine_table, -sine_table]), jnp.stack([sine_table, cosine_table])])

def transform(wave_field, blocks_table):
    table_wide = blocks_table.astype(jnp.float32)
    half_pass = jnp.einsum('abkr,bpmrc->apmkc', table_wide, wave_field.astype(jnp.float32), precision=lax.Precision.HIGHEST)
    half_pass = lax.optimization_barrier(half_pass.astype(jnp.bfloat16)).astype(jnp.float32)
    return jnp.einsum('bpmrc,abck->apmrk', half_pass, table_wide, precision=lax.Precision.HIGHEST)

def complex_times(left_factor, right_factor):
    return jnp.stack([left_factor[0] * right_factor[0] - left_factor[1] * right_factor[1], left_factor[0] * right_factor[1] + left_factor[1] * right_factor[0]])

def conj_times(left_factor, right_factor):
    return jnp.stack([left_factor[0] * right_factor[0] + left_factor[1] * right_factor[1], left_factor[0] * right_factor[1] - left_factor[1] * right_factor[0]])

def amplitude_scaling(model_intensity, measured_block, live_block):
    floored = jnp.maximum(jnp.sqrt(model_intensity), 0.5)
    return live_block[:, None, None] * (1.0 - jnp.sqrt(measured_block) / floored)

def place_terms(accumulated, terms, row_tops, col_lefts):
    window = terms.shape[-1]
    zero_index = jnp.zeros((), jnp.int32)

    def place_one(position, current):
        anchor = (zero_index, row_tops[position], col_lefts[position])
        old_values = lax.dynamic_slice(current, anchor, (2, window, window))
        return lax.dynamic_update_slice(current, old_values + terms[:, position], anchor)
    return lax.fori_loop(0, terms.shape[1], place_one, accumulated)

def reference(object_field, probe_modes, measured, row_starts, col_starts, live_counts):
    forward_blocks = dft_blocks(WIN, 1.0)
    backward_blocks = dft_blocks(WIN, -1.0)
    slot_index = jnp.arange(N_POS, dtype=jnp.int32)
    owner_tile = slot_index // POS_DEV
    row_tops = (owner_tile * TILE_R + row_starts).astype(jnp.int32)
    live_mask = (slot_index % POS_DEV < live_counts[owner_tile]).astype(jnp.float32)
    tiles_count = N_POS // POS_DEV
    tile_items = (row_tops.reshape(tiles_count, POS_DEV), col_starts.astype(jnp.int32).reshape(tiles_count, POS_DEV), live_mask.reshape(tiles_count, POS_DEV), measured.reshape(tiles_count, POS_DEV, WIN, WIN))

    def take_patch(row_top, col_left):
        zero_index = jnp.zeros((), jnp.int32)
        return lax.dynamic_slice(object_field, (zero_index, row_top, col_left), (2, WIN, WIN))

    def advance(running, items_now):
        object_grad, probe_grad = running
        tile_tops, tile_lefts, tile_live, tile_measured = items_now
        patches = jax.vmap(take_patch, in_axes=(0, 0), out_axes=1)(tile_tops, tile_lefts)
        exit_wave = lax.optimization_barrier(complex_times(probe_modes[:, None], patches[:, :, None]).astype(jnp.bfloat16))
        far_field = transform(exit_wave, forward_blocks)
        model_intensity = lax.optimization_barrier(jnp.sum(far_field[0] * far_field[0] + far_field[1] * far_field[1], axis=1))
        scaling = amplitude_scaling(model_intensity, tile_measured, tile_live)
        residual_wave = lax.optimization_barrier((far_field * scaling[None, :, None]).astype(jnp.bfloat16))
        back_wave = transform(residual_wave, backward_blocks)
        object_terms = lax.optimization_barrier(jnp.sum(conj_times(probe_modes[:, None], back_wave), axis=2))
        probe_grad = probe_grad + lax.optimization_barrier(jnp.sum(conj_times(patches[:, :, None], back_wave), axis=1))
        object_grad = place_terms(object_grad, object_terms, tile_tops, tile_lefts)
        return ((object_grad, probe_grad), None)
    start_state = (jnp.zeros(object_field.shape, jnp.float32), jnp.zeros(probe_modes.shape, jnp.float32))
    final_state, unused_out = lax.scan(advance, start_state, tile_items)
    return (final_state[0], final_state[1])
```

```python
import functools
import math

import jax
import jax.numpy as jnp
import numpy as np
from jax import lax
from jax.experimental import pallas as pl
from jax.experimental.pallas import tpu as pltpu
from jax.sharding import PartitionSpec as P


WIN = 256
HALF = 128
F32 = jnp.float32
BF16 = jnp.bfloat16


def tile_perm(move):
    pairs = []
    for t in range(32):
        x, z, c = move(t // 8, t % 8 // 2, t % 2)
        pairs.append((t, x * 8 + z * 2 + c))
    return pairs


def mode_perm(move):
    pairs = []
    for m in range(8):
        z, y = move(m // 4, m % 4)
        pairs.append((m, z * 4 + y))
    return pairs


Y_PLUS = [mode_perm(lambda z, y, k=k: (z, (y + k) % 4)) for k in range(4)]
Z_SWAP = mode_perm(lambda z, y: (1 - z, y))
X_XOR = [tile_perm(lambda x, z, c, k=k: (x ^ k, z, c)) for k in range(4)]
ZLO_XOR = [tile_perm(lambda x, z, c, k=k: (x, z ^ k, c)) for k in range(4)]
CORE_SWAP = tile_perm(lambda x, z, c: (x, z, 1 - c))
TILE_UP = [(i, i + 1) for i in range(31)]
TILE_DOWN = [(i + 1, i) for i in range(31)]


def dft_tables():
    phases = np.outer(np.arange(WIN), np.arange(WIN)) % WIN
    angles = phases * (2.0 * math.pi / WIN)
    scale = 1.0 / math.sqrt(WIN)
    cos_table = jnp.asarray((np.cos(angles) * scale).astype(np.float32)).astype(BF16)
    sin_table = jnp.asarray((-np.sin(angles) * scale).astype(np.float32)).astype(BF16)
    return cos_table, sin_table


def mm(a, b):
    return jnp.dot(a, b, preferred_element_type=F32)


def forward_kernel(sc, above, own, below, p0, p1, p2, p3, cr_ref, ci_ref, patch, far, inten, slab):
    row_top, col = sc[0], sc[1]
    block = jnp.minimum(col // 128, 5)
    lane_shift = col - block * 128
    lane_start = pl.multiple_of(block * 128, 128)
    for src, offset, rows in ((above, 0, HALF), (own, HALF, WIN), (below, HALF + WIN, HALF)):
        for part in range(2):
            wide = src[part, :, pl.ds(lane_start, 384)]
            rolled = pltpu.roll(wide, (384 - lane_shift) % 384, axis=1)
            slab[part, offset : offset + rows, :] = rolled[:, :WIN]
    row_start = pl.multiple_of(row_top // 8 * 8, 8)
    row_shift = row_top - row_start
    for part in range(2):
        tall = slab[part, pl.ds(row_start, WIN + 8), :]
        patch[part] = pltpu.roll(tall, (WIN + 8 - row_shift) % (WIN + 8), axis=0)[:WIN]
    cr, ci = cr_ref[...], ci_ref[...]
    for j, probe in enumerate((p0, p1, p2, p3)):
        pr, pi, qr, qi = probe[0, 0], probe[1, 0], patch[0], patch[1]
        er = (pr * qr - pi * qi).astype(BF16)
        ei = (pr * qi + pi * qr).astype(BF16)
        hr = (mm(cr, er) - mm(ci, ei)).astype(BF16)
        hi = (mm(cr, ei) + mm(ci, er)).astype(BF16)
        fr = mm(hr, cr) - mm(hi, ci)
        fi = mm(hr, ci) + mm(hi, cr)
        far[j, 0] = fr
        far[j, 1] = fi
        power = fr * fr + fi * fi
        inten[...] = power if j == 0 else inten[...] + power


def backward_kernel(first, sc, far, mine, other, meas, patch, p0, p1, p2, p3, cr_ref, ci_ref, *rest):
    if first:
        o0, o1, o2, o3, grad, obj, place = rest
    else:
        prior, o0, o1, o2, o3, grad, obj, place = rest
    row_top, col, live, y = sc[0], sc[1], sc[3], sc[4]
    floored = jnp.maximum(jnp.sqrt(mine[...] + other[...]), 0.5)
    scaling = live.astype(F32) * (1.0 - jnp.sqrt(meas[0]) / floored)
    cr, ci = cr_ref[...], ci_ref[...]
    for j, probe in enumerate((p0, p1, p2, p3)):
        xr = (far[j, 0] * scaling).astype(BF16)
        xi = (far[j, 1] * scaling).astype(BF16)
        hr = (mm(cr, xr) + mm(ci, xi)).astype(BF16)
        hi = (mm(cr, xi) - mm(ci, xr)).astype(BF16)
        br = mm(hr, cr) + mm(hi, ci)
        bi = mm(hi, cr) - mm(hr, ci)
        pr, pi, qr, qi = probe[0, 0], probe[1, 0], patch[0], patch[1]
        o_r = pr * br + pi * bi
        o_i = pr * bi - pi * br
        g_r = qr * br + qi * bi
        g_i = qr * bi - qi * br
        if j == 0:
            obj[0], obj[1] = o_r, o_i
        else:
            obj[0] += o_r
            obj[1] += o_i
        if first:
            grad[j, 0], grad[j, 1] = g_r, g_i
        else:
            grad[j, 0] = prior[j, 0] + g_r
            grad[j, 1] = prior[j, 1] + g_i
    block = col // 128
    lane_shift = col - block * 128
    row_shift = row_top % 8
    for part in range(2):
        wide = jnp.concatenate([obj[part], jnp.zeros((WIN, 128), F32)], axis=1)
        wide = jnp.concatenate([wide, jnp.zeros((8, 384), F32)], axis=0)
        wide = pltpu.roll(wide, lane_shift, axis=1)
        wide = pltpu.roll(wide, row_shift, axis=0)
        place[part, :, :384] = wide
        place[part, :, 384:] = jnp.zeros((WIN + 8, 128), F32)
    for d, out in enumerate((o0, o1, o2, o3)):
        at = lax.rem(y + d - block + 8, 4)
        out[...] = place[:, :, pl.ds(pl.multiple_of(at * 128, 128), 128)]


def gather_kernel(sc, *rest):
    pieces, (mine, other, up, down, acc) = rest[:8], rest[8:]
    acc[...] = jnp.zeros(acc.shape, F32)
    for n, piece in enumerate(pieces):
        start = pl.multiple_of(sc[2 * n], 8)
        which = sc[2 * n + 1]
        acc[which, :, pl.ds(start, WIN + 8), :] += piece[...]
    mine[...] = acc[0, :, HALF : HALF + WIN]
    other[...] = acc[1, :, HALF : HALF + WIN]
    up[...] = acc[:, :, :HALF]
    down[...] = acc[:, :, HALF + WIN : 2 * HALF + WIN]


def call(kernel, n_in, outs, scratch, measured_at=None):
    def whole(shape):
        return pl.BlockSpec(shape, lambda g, s, n=len(shape): (0,) * n)

    def run(scalars, *arrays):
        in_specs = []
        for i, a in enumerate(arrays):
            if i == measured_at:
                in_specs.append(pl.BlockSpec((1, WIN, WIN), lambda g, s: (s[2], 0, 0)))
            else:
                in_specs.append(whole(a.shape))
        return pl.pallas_call(
            kernel,
            out_shape=[jax.ShapeDtypeStruct(s, F32) for s in outs],
            grid_spec=pltpu.PrefetchScalarGridSpec(
                num_scalar_prefetch=1,
                grid=(1,),
                in_specs=in_specs,
                out_specs=[whole(s) for s in outs],
                scratch_shapes=[pltpu.VMEM(s, F32) for s in scratch],
            ),
        )(scalars, *arrays)

    return run


def body(object_field, probe_modes, measured, row_starts, col_starts, live_counts):
    mode = lax.axis_index("mode")
    tile = lax.axis_index("tile")
    z_hi, y = mode // 4, mode % 4
    x, core = tile // 8, tile % 2
    row_tops = row_starts + HALF
    cr, ci = dft_tables()

    above = lax.ppermute(object_field[:, WIN - HALF :], "tile", TILE_UP)
    below = lax.ppermute(object_field[:, :HALF], "tile", TILE_DOWN)
    probes = [probe_modes] + [lax.ppermute(probe_modes, "mode", Y_PLUS[k]) for k in (1, 2, 3)]

    def slot_scalars(i):
        slot = y * 2 + i
        live = (slot < live_counts[0]).astype(jnp.int32)
        return jnp.stack([row_tops[slot], col_starts[slot], slot, live, y]).astype(jnp.int32)

    scalars = [slot_scalars(i) for i in range(2)]
    forward = call(
        forward_kernel,
        9,
        [(2, WIN, WIN), (4, 2, WIN, WIN), (WIN, WIN)],
        [(2, 2 * WIN + 8, WIN)],
    )
    fwd = [forward(scalars[i], above, object_field, below, *probes, cr, ci) for i in range(2)]
    others = [lax.ppermute(fwd[i][2], "mode", Z_SWAP) for i in range(2)]

    pieces, grad = [], None
    for i in range(2):
        patch, far, mine = fwd[i]
        backward = call(
            functools.partial(backward_kernel, i == 0),
            12,
            [(2, WIN + 8, 128)] * 4 + [(4, 2, WIN, WIN)],
            [(2, WIN, WIN), (2, WIN + 8, 512)],
            measured_at=3,
        )
        extra = [] if i == 0 else [grad]
        *parts, grad = backward(
            scalars[i], far, mine, others[i], measured, patch, *probes, cr, ci, *extra
        )
        pieces.append(parts[:1] + [lax.ppermute(parts[d], "mode", Y_PLUS[d]) for d in (1, 2, 3)])

    halves = grad.reshape(4, 2, 2, HALF, WIN)
    send = lax.dynamic_index_in_dim(halves, 1 - core, 2, keepdims=False)
    keep = lax.dynamic_index_in_dim(halves, core, 2, keepdims=False)
    summed = keep + lax.ppermute(send, "tile", CORE_SWAP)
    quarters = summed.reshape(4, 2, 4, 32, WIN)
    total = lax.dynamic_index_in_dim(quarters, x, 2, keepdims=False)
    arrived = [
        lax.ppermute(lax.dynamic_index_in_dim(quarters, x ^ k, 2, keepdims=False), "tile", X_XOR[k])
        for k in (1, 2, 3)
    ]
    total = (total + arrived[0]) + (arrived[1] + arrived[2])
    back = [lax.ppermute(total[k], "mode", Y_PLUS[4 - k]) for k in (1, 2, 3)]
    total = (total[0] + back[0]) + (back[1] + back[2])
    along = [lax.ppermute(total, "tile", ZLO_XOR[k]) for k in (1, 2, 3)]
    total = (total + along[0]) + (along[1] + along[2])
    chunks = [total] + [lax.ppermute(total, "tile", X_XOR[k]) for k in (1, 2, 3)]
    stacked = jnp.stack(chunks, axis=1)
    order = jnp.arange(4) ^ x
    half = jnp.take(stacked, order, axis=1).reshape(2, HALF, WIN)
    partner = lax.ppermute(half, "tile", CORE_SWAP)
    first = jnp.where(core == 0, half, partner)
    second = jnp.where(core == 0, partner, half)
    probe_grad = jnp.concatenate([first, second], axis=1)[:, None]

    entries = []
    flat = []
    for i in range(2):
        for d in range(4):
            slot = (y + 4 - d) % 4 * 2 + i
            block = col_starts[slot] // 128
            low = (y >= block) & (y <= block + 2)
            owner = jnp.where(low, 0, 1)
            entries += [row_tops[slot] // 8 * 8, owner ^ z_hi]
            flat.append(pieces[i][d])
    gather = call(
        gather_kernel,
        8,
        [(2, WIN, 128), (2, WIN, 128), (2, 2, HALF, 128), (2, 2, HALF, 128)],
        [(2, 2, 2 * WIN + 8, 128)],
    )
    mine, other, up, down = gather(jnp.stack(entries).astype(jnp.int32), *flat)
    from_next = lax.ppermute(up, "tile", TILE_DOWN)
    from_prev = lax.ppermute(down, "tile", TILE_UP)
    other = other + jnp.concatenate([from_prev[1], from_next[1]], axis=1)
    crossed = lax.ppermute(other, "mode", Z_SWAP)
    mine = mine + jnp.concatenate([from_prev[0], from_next[0]], axis=1)
    object_grad = mine + crossed
    return (object_grad, probe_grad)


def solution(mesh):
    return jax.shard_map(
        body,
        mesh=mesh,
        in_specs=(
            P(None, "tile", None),
            P(None, "mode", None, None),
            P("tile", None, None),
            P("tile"),
            P("tile"),
            P("tile"),
        ),
        out_specs=(P(None, "tile", "mode"), P(None, "mode", None, None)),
        check_vma=False,
    )
```

```python
import functools
import math

import jax
import jax.numpy as jnp
import numpy as np
from jax import lax
from jax.experimental import pallas as pl
from jax.experimental.pallas import tpu as pltpu
from jax.sharding import PartitionSpec as P


WIN = 256
HALF = 128
F32 = jnp.float32
BF16 = jnp.bfloat16


def tile_perm(move):
    pairs = []
    for t in range(32):
        x, z, c = move(t // 8, t % 8 // 2, t % 2)
        pairs.append((t, x * 8 + z * 2 + c))
    return pairs


def mode_perm(move):
    pairs = []
    for m in range(8):
        z, y = move(m // 4, m % 4)
        pairs.append((m, z * 4 + y))
    return pairs


Y_PLUS = [mode_perm(lambda z, y, k=k: (z, (y + k) % 4)) for k in range(4)]
Z_SWAP = mode_perm(lambda z, y: (1 - z, y))
X_XOR = [tile_perm(lambda x, z, c, k=k: (x ^ k, z, c)) for k in range(4)]
ZLO_XOR = [tile_perm(lambda x, z, c, k=k: (x, z ^ k, c)) for k in range(4)]
CORE_SWAP = tile_perm(lambda x, z, c: (x, z, 1 - c))


def tile_step(step):
    pairs = []
    for t in range(max(0, -step), min(32, 32 - step)):
        crosses = abs(t % 8 - (t + step) % 8) == 7
        for m in range(8):
            pairs.append((t * 8 + m, (t + step) * 8 + (m ^ 4 if crosses else m)))
    return pairs


BOTH = ("tile", "mode")
TILE_UP = tile_step(1)
TILE_DOWN = tile_step(-1)


def dft_tables():
    phases = np.outer(np.arange(WIN), np.arange(WIN)) % WIN
    angles = phases * (2.0 * math.pi / WIN)
    scale = 1.0 / math.sqrt(WIN)
    cos_table = jnp.asarray((np.cos(angles) * scale).astype(np.float32)).astype(BF16)
    sin_table = jnp.asarray((-np.sin(angles) * scale).astype(np.float32)).astype(BF16)
    return cos_table, sin_table


def mm(a, b):
    return jnp.dot(a, b, preferred_element_type=F32)


def load_all(pairs, sem, first=0):
    copies = [pltpu.make_async_copy(s, d, sem.at[first + n]) for n, (s, d) in enumerate(pairs)]
    for c in copies:
        c.start()
    return copies


def wait_all(copies):
    for c in copies:
        c.wait()


def start_kernel(tile, own, probe, last, lead, part, b0, b1, b2, sem):
    core = pl.multiple_of((tile[0] & 1) * HALF, HALF)
    loads = load_all(
        [(probe.at[:, 0, pl.ds(core, HALF)], b2), (own.at[:, WIN - HALF :], b0), (own.at[:, :HALF], b1)], sem
    )
    stores = []
    for n, pair in enumerate(((b2, part), (b0, last), (b1, lead))):
        loads[n].wait()
        stores += load_all([pair], sem, 3 + n)
    wait_all(stores)


def table_kernel(cr_in, ci_in, left_out, right_out, cr_ref, ci_ref, left, right, sem):
    wait_all(load_all([(cr_in, cr_ref), (ci_in, ci_ref)], sem))
    cr, ci = cr_ref[...], ci_ref[...]
    left[:WIN, :WIN] = cr
    left[:WIN, WIN:] = -ci
    left[WIN:, :WIN] = ci
    left[WIN:, WIN:] = cr
    right[:WIN, :WIN] = cr
    right[:WIN, WIN:] = ci
    right[WIN:, :WIN] = -ci
    right[WIN:, WIN:] = cr
    wait_all(load_all([(left, left_out), (right, right_out)], sem, 2))


def two_passes(re, im, rows_table, cols_table):
    stacked = jnp.concatenate([re, im], axis=0)
    half = mm(rows_table[...], stacked).astype(BF16)
    return mm(jnp.concatenate([half[:WIN], half[WIN:]], axis=1), cols_table[...])


def probe_loads(core, p0, parts, probes):
    near = pl.multiple_of(core * HALF, HALF)
    far = pl.multiple_of((1 - core) * HALF, HALF)
    pairs = [(p0.at[:, 0], probes.at[0])]
    for j in range(3):
        pairs.append((parts[j], probes.at[j + 1, :, pl.ds(near, HALF)]))
        pairs.append((parts[3 + j], probes.at[j + 1, :, pl.ds(far, HALF)]))
    return pairs


def forward_kernel(i, mode, tile, rows, cols, left_in, right_in, above, own, below, p0, *rest):
    parts, rest = rest[:6], rest[6:]
    patch, far, inten, slab, probes, far_out, acc, out, left, right, sem_in, sem_p, sem_out = rest
    slot = (mode[0] & 3) * 2 + i
    row_top, col = rows[slot] + HALF, cols[slot]
    block = jnp.minimum(col // 128, 5)
    lane_shift = col - block * 128
    lane_start = pl.multiple_of(block * 128, 128)
    windows = load_all(
        [
            (src.at[:, :, pl.ds(lane_start, 384)], slab.at[:, pl.ds(offset, size), :])
            for src, offset, size in ((above, 0, HALF), (own, HALF, WIN), (below, HALF + WIN, HALF))
        ],
        sem_in,
    )
    loads = load_all([(left_in, left), (right_in, right)] + probe_loads(tile[0] & 1, p0, parts, probes), sem_p)
    wait_all(windows)
    row_start = pl.multiple_of(row_top // 8 * 8, 8)
    row_shift = row_top - row_start
    for part in range(2):
        tall = slab[part, pl.ds(row_start, WIN + 8), :]
        tall = pltpu.roll(tall, (WIN + 8 - row_shift) % (WIN + 8), axis=0)[:WIN]
        out[part] = pltpu.roll(tall, (384 - lane_shift) % 384, axis=1)[:, :WIN]
    wait_all(loads)
    stores = load_all([(out, patch)], sem_out)
    for j in range(4):
        pr, pi, qr, qi = probes[j, 0], probes[j, 1], out[0], out[1]
        er = (pr * qr - pi * qi).astype(BF16)
        ei = (pr * qi + pi * qr).astype(BF16)
        both = two_passes(er, ei, left, right)
        far_out[j] = both
        power = both[:, :WIN] * both[:, :WIN] + both[:, WIN:] * both[:, WIN:]
        acc[...] = power if j == 0 else acc[...] + power
        if j % 2:
            stores += load_all([(far_out.at[pl.ds(j - 1, 2)], far.at[pl.ds(j - 1, 2)])], sem_out, 1 + j // 2)
    stores += load_all([(acc, inten)], sem_out, 3)
    wait_all(stores)


def backward_kernel(i, mode, tile, rows, cols, live, left_in, right_in, mine, other, meas, patch_in, far, p0, *rest):
    parts, rest = rest[:6], rest[6:]
    if i:
        prior, rest = rest[0], rest[1:]
        rest = rest[4:]
    outs, rest = rest[:4], rest[4:]
    grads, rest = rest[: 1 + i], rest[1 + i :]
    obj, place, patch, probes, far_in, grad_out, inten, left, right, sem_i, sem_f, sem_out = rest
    core = tile[0] & 1
    y = mode[0] & 3
    slot = y * 2 + i
    row_top, col = rows[slot] + HALF, cols[slot]
    early = load_all([(mine, inten.at[0]), (other, inten.at[1]), (meas.at[slot], inten.at[2])], sem_i)
    pairs = [(left_in, left), (right_in, right), (patch_in, patch), (far, far_in)]
    pairs += probe_loads(core, p0, parts, probes)
    if i:
        pairs.append((prior, grad_out))
    loads = load_all(pairs, sem_f)
    wait_all(early)
    alive = (slot < live[0]).astype(F32)
    floored = jnp.maximum(jnp.sqrt(inten[0] + inten[1]), 0.5)
    inten[2] = alive * (1.0 - jnp.sqrt(inten[2]) / floored)
    wait_all(loads)
    stores = []
    near = pl.multiple_of(core * HALF, HALF)
    away = pl.multiple_of((1 - core) * HALF, HALF)
    for j in range(4):
        scaling = inten[2]
        xr = (far_in[j, :, :WIN] * scaling).astype(BF16)
        xi = (far_in[j, :, WIN:] * scaling).astype(BF16)
        both = two_passes(xr, xi, right, left)
        br, bi = both[:, :WIN], both[:, WIN:]
        pr, pi, qr, qi = probes[j, 0], probes[j, 1], patch[0], patch[1]
        o_r = pr * br + pi * bi
        o_i = pr * bi - pi * br
        g_r = qr * br + qi * bi
        g_i = qr * bi - qi * br
        if j == 0:
            obj[0], obj[1] = o_r, o_i
        else:
            obj[0] += o_r
            obj[1] += o_i
        if i == 0:
            grad_out[j, 0], grad_out[j, 1] = g_r, g_i
        else:
            grad_out[j, 0] += g_r
            grad_out[j, 1] += g_i
    if i == 0:
        stores += load_all([(grad_out, grads[0])], sem_out)
    else:
        stores += load_all(
            [(grad_out.at[:, :, pl.ds(near, HALF)], grads[0]), (grad_out.at[:, :, pl.ds(away, HALF)], grads[1])],
            sem_out,
        )
    block = col // 128
    lane_shift = col - block * 128
    row_shift = row_top & 7
    for part in range(2):
        wide = jnp.concatenate([obj[part], jnp.zeros((WIN, 128), F32)], axis=1)
        place[part, :WIN, :384] = pltpu.roll(wide, lane_shift, axis=1)
        place[part, WIN:, :] = jnp.zeros((8, 512), F32)
        place[part, :WIN, 384:] = jnp.zeros((WIN, 128), F32)
        for n in range(3):
            at = slice(128 * n, 128 * n + 128)
            place[part, :, at] = pltpu.roll(place[part, :, at], row_shift, axis=0)
    pairs = []
    for d, out in enumerate(outs):
        at = pl.multiple_of(((y + d - block + 8) & 3) * 128, 128)
        pairs.append((place.at[:, :, pl.ds(at, 128)], out.at[i]))
    stores += load_all(pairs, sem_out, 2)
    wait_all(stores)


def gather_kernel(mode, rows, cols, *rest):
    pieces, (mine, other, up, down, acc, buf, sem_in, sem_out) = rest[:4], rest[4:]
    loads = load_all([(p, buf.at[n]) for n, p in enumerate(pieces)], sem_in)
    acc[...] = jnp.zeros(acc.shape, F32)
    y, z_hi = mode[0] & 3, mode[0] >> 2
    wait_all(loads)
    for n in range(8):
        i, d = n % 2, n // 2
        slot = ((y + 4 - d) & 3) * 2 + i
        block = cols[slot] // 128
        low = jnp.logical_and(y >= block, y <= block + 2)
        which = jnp.where(low, 0, 1)
        start = pl.multiple_of((rows[slot] + HALF) // 8 * 8, 8)
        acc[which, :, pl.ds(start, WIN + 8), :] += buf[d, i]
    wait_all(
        load_all(
            [
                (acc.at[:, :, pl.ds(0, HALF)], up),
                (acc.at[:, :, pl.ds(HALF + WIN, HALF)], down),
                (acc.at[z_hi, :, pl.ds(HALF, WIN)], mine),
                (acc.at[1 - z_hi, :, pl.ds(HALF, WIN)], other),
            ],
            sem_out,
        )
    )


def split_kernel(tile, keep, arrived, *rest):
    outs, (total, addend, sem_in, sem_out) = rest[:4], rest[4:]
    x = tile[0] >> 3
    loads = []
    for k in range(4):
        at = pl.multiple_of((x ^ k) * 32, 32)
        pairs = [(keep.at[:, :, pl.ds(at, 32)], total.at[k]), (arrived.at[:, :, pl.ds(at, 32)], addend.at[k])]
        loads.append(load_all(pairs, sem_in, 2 * k))
    stores = []
    for k in (1, 2, 3, 0):
        wait_all(loads[k])
        total[k] += addend[k]
        stores += load_all([(total.at[k], outs[k])], sem_out, k)
    wait_all(stores)


SMEM = pl.BlockSpec(memory_space=pltpu.SMEM)
HBM = pl.BlockSpec(memory_space=pltpu.HBM)
DMA = pltpu.SemaphoreType.DMA
TABLE = (2 * WIN, 2 * WIN)


def kernel_call(kernel, scalars, arrays, outs, scratch, vmem_mib, aliases=()):
    return pl.pallas_call(
        kernel,
        out_shape=[pltpu.HBM(s, t) for s, t in outs],
        in_specs=[SMEM] * len(scalars) + [HBM] * len(arrays),
        out_specs=[HBM] * len(outs),
        scratch_shapes=scratch,
        compiler_params=pltpu.CompilerParams(vmem_limit_bytes=vmem_mib << 20),
        input_output_aliases=dict(aliases),
    )(*scalars, *arrays)


def start_call(tile, own, probe):
    shapes = [(2, HALF, 1024), (2, HALF, 1024), (2, HALF, WIN)]
    return kernel_call(start_kernel, (tile,), (own, probe), [(s, F32) for s in shapes],
        [pltpu.VMEM(s, F32) for s in shapes] + [DMA((6,))], 8)


def table_call():
    quarter = pltpu.VMEM((WIN, WIN), BF16)
    whole = pltpu.VMEM(TABLE, BF16)
    tables = [stay(t) for t in dft_tables()]
    return kernel_call(table_kernel, (), tables, [(TABLE, BF16)] * 2, [quarter, quarter, whole, whole, DMA((4,))], 6)


def forward_call(i, scalars, tables, fields, probes):
    return kernel_call(
        functools.partial(forward_kernel, i),
        scalars,
        (*tables, *fields, *probes),
        [((2, WIN, WIN), F32), ((4, WIN, 2 * WIN), F32), ((WIN, WIN), F32)],
        [
            pltpu.VMEM((2, 2 * WIN + 8, 384), F32),
            pltpu.VMEM((4, 2, WIN, WIN), F32),
            pltpu.VMEM((4, WIN, 2 * WIN), F32),
            pltpu.VMEM((WIN, WIN), F32),
            pltpu.VMEM((2, WIN, WIN), F32),
            pltpu.VMEM(TABLE, BF16),
            pltpu.VMEM(TABLE, BF16),
            DMA((3,)),
            DMA((9,)),
            DMA((4,)),
        ],
        28,
    )


def backward_call(i, scalars, tables, mine, other, measured, patch, far, probes, prior):
    window = (2, 2, WIN + 8, 128)
    grads = [((4, 2, WIN, WIN), F32)] if i == 0 else [((4, 2, HALF, WIN), F32)] * 2
    return kernel_call(
        functools.partial(backward_kernel, i),
        scalars,
        (*tables, mine, other, measured, patch, far, *probes, *prior),
        [(window, F32)] * 4 + grads,
        [
            pltpu.VMEM((2, WIN, WIN), F32),
            pltpu.VMEM((2, WIN + 8, 512), F32),
            pltpu.VMEM((2, WIN, WIN), F32),
            pltpu.VMEM((4, 2, WIN, WIN), F32),
            pltpu.VMEM((4, WIN, 2 * WIN), F32),
            pltpu.VMEM((4, 2, WIN, WIN), F32),
            pltpu.VMEM((3, WIN, WIN), F32),
            pltpu.VMEM(TABLE, BF16),
            pltpu.VMEM(TABLE, BF16),
            DMA((3,)),
            DMA((12,)),
            DMA((6,)),
        ],
        32,
        () if i == 0 else [(len(scalars) + 15 + n, n) for n in range(4)],
    )


def gather_call(scalars, pieces):
    shapes = [(2, WIN, 128), (2, WIN, 128), (2, 2, HALF, 128), (2, 2, HALF, 128)]
    return kernel_call(
        gather_kernel,
        scalars,
        pieces,
        [(s, F32) for s in shapes],
        [pltpu.VMEM((2, 2, 2 * WIN + 8, 128), F32), pltpu.VMEM((4, 2, 2, WIN + 8, 128), F32), DMA((4,)), DMA((4,))],
        16,
    )


def split_call(tile, keep, arrived):
    chunk = (4, 2, 32, WIN)
    return kernel_call(
        split_kernel,
        (tile,),
        (keep, arrived),
        [(chunk, F32)] * 4,
        [pltpu.VMEM((4, *chunk), F32), pltpu.VMEM((4, *chunk), F32), DMA((8,)), DMA((4,))],
        12,
    )


def stay(value):
    return pltpu.with_memory_space_constraint(value, pltpu.HBM)


def gradients(object_field, probe_modes, measured, row_starts, col_starts, live_counts):
    mode_index = lax.axis_index("mode").astype(jnp.int32)
    tile_index = lax.axis_index("tile").astype(jnp.int32)
    x, core = tile_index // 8, tile_index % 2
    mode, tile = mode_index.reshape(1), tile_index.reshape(1)
    scalars = (mode, tile, row_starts, col_starts)

    last, lead, part = start_call(tile, stay(object_field), stay(probe_modes))
    above = lax.ppermute(last, BOTH, TILE_UP)
    below = lax.ppermute(lead, BOTH, TILE_DOWN)
    near = [lax.ppermute(part, "mode", Y_PLUS[k]) for k in (1, 2, 3)]
    away = [lax.ppermute(near[k - 1], "tile", CORE_SWAP) for k in (1, 2, 3)]
    probes = [stay(probe_modes), *near, *away]
    tables = [stay(t) for t in table_call()]

    fields = (above, stay(object_field), below)
    fwd = [forward_call(i, scalars, tables, fields, probes) for i in range(2)]
    others = [lax.ppermute(fwd[i][2], "mode", Z_SWAP) for i in range(2)]

    prior = []
    for i in range(2):
        patch, far, mine = [stay(a) for a in fwd[i]]
        outs = backward_call(
            i, (*scalars, live_counts), tables, mine, others[i], stay(measured), patch, far, probes, prior
        )
        parts, grads = list(outs[:4]), [stay(g) for g in outs[4:]]
        prior = [*grads, *map(stay, parts)]
    pieces = [stay(parts[0])] + [lax.ppermute(parts[d], "mode", Y_PLUS[d]) for d in (1, 2, 3)]

    keep, give = grads[0], outs[5]
    arrived = lax.ppermute(give, "tile", CORE_SWAP)
    chunks = split_call(tile, keep, arrived)
    back = [lax.ppermute(chunks[k], "tile", X_XOR[k]) for k in (1, 2, 3)]
    total = (chunks[0] + back[0]) + (back[1] + back[2])
    back = [lax.ppermute(total[k], "mode", Y_PLUS[4 - k]) for k in (1, 2, 3)]
    total = (total[0] + back[0]) + (back[1] + back[2])
    back = [lax.ppermute(total, "tile", ZLO_XOR[k]) for k in (1, 2, 3)]
    total = (total + back[0]) + (back[1] + back[2])
    rows = [total] + [lax.ppermute(total, "tile", X_XOR[k]) for k in (1, 2, 3)]
    half = jnp.take(jnp.stack(rows, axis=1), jnp.arange(4) ^ x, axis=1).reshape(2, HALF, WIN)
    partner = lax.ppermute(half, "tile", CORE_SWAP)
    first = jnp.where(core == 0, half, partner)
    second = jnp.where(core == 0, partner, half)
    probe_grad = jnp.concatenate([first, second], axis=1)[:, None]

    mine, other, up, down = gather_call((mode, row_starts, col_starts), pieces)
    from_next = lax.ppermute(up, BOTH, TILE_DOWN)
    from_prev = lax.ppermute(down, BOTH, TILE_UP)
    z_hi = mode_index // 4

    def rims(which):
        above = lax.dynamic_index_in_dim(from_prev, which, 0, keepdims=False)
        below = lax.dynamic_index_in_dim(from_next, which, 0, keepdims=False)
        return jnp.concatenate([above, below], axis=1)

    crossed = lax.ppermute(other + rims(1 - z_hi), "mode", Z_SWAP)
    object_grad = (mine + rims(z_hi)) + crossed
    return (object_grad, probe_grad)


def solution(mesh):
    return jax.shard_map(
        gradients,
        mesh=mesh,
        in_specs=(
            P(None, "tile", None),
            P(None, "mode", None, None),
            P("tile", None, None),
            P("tile"),
            P("tile"),
            P("tile"),
        ),
        out_specs=(P(None, "tile", "mode"), P(None, "mode", None, None)),
        check_vma=False,
    )
```

```python
import functools
import math

import jax
import jax.numpy as jnp
import numpy as np
from jax import lax
from jax.experimental import pallas as pl
from jax.experimental.pallas import tpu as pltpu
from jax.sharding import PartitionSpec as P


WIN = 256
HALF = 128
F32 = jnp.float32
BF16 = jnp.bfloat16


def tile_perm(move):
    pairs = []
    for t in range(32):
        x, z, c = move(t // 8, t % 8 // 2, t % 2)
        pairs.append((t, x * 8 + z * 2 + c))
    return pairs


def mode_perm(move):
    pairs = []
    for m in range(8):
        z, y = move(m // 4, m % 4)
        pairs.append((m, z * 4 + y))
    return pairs


Y_PLUS = [mode_perm(lambda z, y, k=k: (z, (y + k) % 4)) for k in range(4)]
Z_SWAP = mode_perm(lambda z, y: (1 - z, y))
X_XOR = [tile_perm(lambda x, z, c, k=k: (x ^ k, z, c)) for k in range(4)]
ZLO_XOR = [tile_perm(lambda x, z, c, k=k: (x, z ^ k, c)) for k in range(4)]
CORE_SWAP = tile_perm(lambda x, z, c: (x, z, 1 - c))


def tile_step(step):
    pairs = []
    for t in range(max(0, -step), min(32, 32 - step)):
        crosses = abs(t % 8 - (t + step) % 8) == 7
        for m in range(8):
            pairs.append((t * 8 + m, (t + step) * 8 + (m ^ 4 if crosses else m)))
    return pairs


BOTH = ("tile", "mode")
TILE_UP = tile_step(1)
TILE_DOWN = tile_step(-1)


def dft_tables():
    phases = np.outer(np.arange(WIN), np.arange(WIN)) % WIN
    angles = phases * (2.0 * math.pi / WIN)
    scale = 1.0 / math.sqrt(WIN)
    cos_table = jnp.asarray((np.cos(angles) * scale).astype(np.float32)).astype(BF16)
    sin_table = jnp.asarray((-np.sin(angles) * scale).astype(np.float32)).astype(BF16)
    return cos_table, sin_table


def mm(a, b):
    return jnp.dot(a, b, preferred_element_type=F32)


def load_all(pairs, sem, first=0):
    copies = [pltpu.make_async_copy(s, d, sem.at[first + n]) for n, (s, d) in enumerate(pairs)]
    for c in copies:
        c.start()
    return copies


def wait_all(copies):
    for c in copies:
        c.wait()


def start_kernel(tile, own, probe, last, lead, part, sem):
    core = pl.multiple_of((tile[0] & 1) * HALF, HALF)
    wait_all(
        load_all(
            [(probe.at[:, 0, pl.ds(core, HALF)], part), (own.at[:, WIN - HALF :], last), (own.at[:, :HALF], lead)], sem
        )
    )


def table_kernel(cr_in, ci_in, left, right, cr_ref, ci_ref, sem):
    wait_all(load_all([(cr_in, cr_ref), (ci_in, ci_ref)], sem))
    cr, ci = cr_ref[...], ci_ref[...]
    left[:WIN, :WIN] = cr
    left[:WIN, WIN:] = -ci
    left[WIN:, :WIN] = ci
    left[WIN:, WIN:] = cr
    right[:WIN, :WIN] = cr
    right[:WIN, WIN:] = ci
    right[WIN:, :WIN] = -ci
    right[WIN:, WIN:] = cr


def rows_from(tall, shift):
    n, lanes = tall.shape
    tiles = pltpu.roll(tall.reshape(n // 8, 8, lanes), (8 - shift) & 7, axis=1)
    row = lax.broadcasted_iota(jnp.int32, (n // 8 - 1, 8, lanes), 1)
    return jnp.where(row < 8 - shift, tiles[:-1], tiles[1:]).reshape(n - 8, lanes)


def lanes_from(wide, shift):
    tiles = [pltpu.roll(wide[:, 128 * t : 128 * t + 128], (128 - shift) & 127, axis=1) for t in range(3)]
    lane = lax.broadcasted_iota(jnp.int32, tiles[0].shape, 1)
    return jnp.concatenate([jnp.where(lane < 128 - shift, tiles[t], tiles[t + 1]) for t in range(2)], axis=1)


def rows_to(flat, shift):
    n, lanes = flat.shape
    tiles = pltpu.roll(flat.reshape(n // 8, 8, lanes), shift, axis=1)
    none = jnp.zeros((1, 8, lanes), F32)
    row = lax.broadcasted_iota(jnp.int32, (n // 8 + 1, 8, lanes), 1)
    moved = jnp.where(row < shift, jnp.concatenate([none, tiles]), jnp.concatenate([tiles, none]))
    return moved.reshape(n + 8, lanes)


def two_passes(stacked, rows_table, cols_table):
    half = mm(rows_table[...], stacked).astype(BF16)
    return mm(jnp.concatenate([half[:WIN], half[WIN:]], axis=1), cols_table[...])


def probe_of(j, core, own, parts):
    if j == 0:
        return own[0], own[1]
    near, away = parts[j - 1], parts[j + 2]
    swapped = core == 1
    return [
        jnp.concatenate(
            [jnp.where(swapped, away[n], near[n]), jnp.where(swapped, near[n], away[n])], axis=0
        )
        for n in range(2)
    ]


def forward_kernel(i, mode, tile, rows, cols, left, right, above, own, below, p0, *rest):
    parts, rest = rest[:6], rest[6:]
    out, far, acc, slab, own_probe, sem = rest
    slot = (mode[0] & 3) * 2 + i
    row_top, col = rows[slot] + HALF, cols[slot]
    block = jnp.minimum(col // 128, 5)
    lane_start = pl.multiple_of(block * 128, 128)
    windows = load_all(
        [
            (src.at[:, :, pl.ds(lane_start, 384)], slab.at[:, pl.ds(offset, size), pl.ds(0, 384)])
            for src, offset, size in ((above, 0, HALF), (own, HALF, WIN), (below, HALF + WIN, HALF))
        ],
        sem,
    )
    loads = load_all([(p0.at[:, 0], own_probe)], sem, 3)
    wait_all(windows)
    row_start = pl.multiple_of(row_top // 8 * 8, 8)
    first_lane = pl.multiple_of(col // 128 * 128 - lane_start, 128)
    for part in range(2):
        tall = slab[part, pl.ds(row_start, WIN + 8), pl.ds(first_lane, 384)]
        out[part] = lanes_from(rows_from(tall, row_top & 7), col & 127)
    wait_all(loads)
    for j in range(4):
        (pr, pi), qr, qi = probe_of(j, tile[0] & 1, own_probe, parts), out[0], out[1]
        er = (pr * qr - pi * qi).astype(BF16)
        ei = (pr * qi + pi * qr).astype(BF16)
        both = two_passes(jnp.concatenate([er, ei], axis=0), left, right)
        far[j] = both
        power = both[:, :WIN] * both[:, :WIN] + both[:, WIN:] * both[:, WIN:]
        acc[...] = power if j == 0 else acc[...] + power


def backward_kernel(i, mode, tile, rows, cols, live, left, right, mine, other, meas, patch, far, p0, *rest):
    parts, rest = rest[:6], rest[6:]
    if i:
        prior, rest = rest[0], rest[1:]
    outs, rest = rest[:4], rest[4:]
    grads, rest = rest[: 1 + i], rest[1 + i :]
    obj, place, own_probe, inten, sem = rest
    core = tile[0] & 1
    y = mode[0] & 3
    slot = y * 2 + i
    row_top, col = rows[slot] + HALF, cols[slot]
    loads = load_all([(meas.at[slot], inten), (p0.at[:, 0], own_probe)], sem)
    wait_all(loads)
    alive = (slot < live[0]).astype(F32)
    floored = jnp.maximum(jnp.sqrt(mine[...] + other[...]), 0.5)
    inten[...] = alive * (1.0 - jnp.sqrt(inten[...]) / floored)
    for j in range(4):
        scaling = inten[...]
        xr = (far[j, :, :WIN] * scaling).astype(BF16)
        xi = (far[j, :, WIN:] * scaling).astype(BF16)
        both = two_passes(jnp.concatenate([xr, xi], axis=0), right, left)
        br, bi = both[:, :WIN], both[:, WIN:]
        (pr, pi), qr, qi = probe_of(j, core, own_probe, parts), patch[0], patch[1]
        o_r = pr * br + pi * bi
        o_i = pr * bi - pi * br
        g_r = qr * br + qi * bi
        g_i = qr * bi - qi * br
        if j == 0:
            obj[0], obj[1] = o_r, o_i
        else:
            obj[0] += o_r
            obj[1] += o_i
        for n, g in enumerate((g_r, g_i)):
            if i == 0:
                grads[0][j, n] = g
            else:
                g = g + prior[j, n]
                grads[0][j, n] = jnp.where(core == 1, g[HALF:], g[:HALF])
                grads[1][j, n] = jnp.where(core == 1, g[:HALF], g[HALF:])
    block, lane_shift, row_shift = col // 128, col & 127, row_top & 7
    lane = lax.broadcasted_iota(jnp.int32, (WIN, 128), 1)
    for part in range(2):
        before = jnp.zeros((WIN, 128), F32)
        for n in range(3):
            moved = pltpu.roll(obj[part, :, 128 * n : 128 * n + 128], lane_shift, axis=1) if n < 2 else jnp.zeros_like(before)
            place[part, :, 128 * n : 128 * n + 128] = rows_to(jnp.where(lane < lane_shift, before, moved), row_shift)
            before = moved
        place[part, :, 384:] = jnp.zeros((WIN + 8, 128), F32)
    for d, out in enumerate(outs):
        at = pl.multiple_of(((y + d - block + 8) & 3) * 128, 128)
        out[...] = place[:, :, pl.ds(at, 128)]


def gather_kernel(mode, rows, cols, *rest):
    pieces, (mine, other, up, down, acc) = rest[:8], rest[8:]
    acc[...] = jnp.zeros(acc.shape, F32)
    y, z_hi = mode[0] & 3, mode[0] >> 2
    for n, piece in enumerate(pieces):
        i, d = n // 4, n % 4
        slot = ((y + 4 - d) & 3) * 2 + i
        block = cols[slot] // 128
        low = jnp.logical_and(y >= block, y <= block + 2)
        which = jnp.where(low, 0, 1)
        start = pl.multiple_of((rows[slot] + HALF) // 8 * 8, 8)
        acc[which, :, pl.ds(start, WIN + 8), :] += piece[...]
    mine[...] = acc[z_hi, :, HALF : HALF + WIN]
    other[...] = acc[1 - z_hi, :, HALF : HALF + WIN]
    up[...] = acc[:, :, :HALF]
    down[...] = acc[:, :, HALF + WIN : 2 * HALF + WIN]


def split_kernel(tile, keep, arrived, *outs):
    x = tile[0] >> 3
    for k, out in enumerate(outs):
        at = pl.ds(pl.multiple_of((x ^ k) * 32, 32), 32)
        out[...] = keep[:, :, at] + arrived[:, :, at]


SMEM = pl.BlockSpec(memory_space=pltpu.SMEM)
VMEM = pl.BlockSpec(memory_space=pltpu.VMEM)
HBM = pl.BlockSpec(memory_space=pltpu.HBM)
DMA = pltpu.SemaphoreType.DMA
TABLE = (2 * WIN, 2 * WIN)


def kernel_call(kernel, scalars, arrays, outs, scratch, vmem_mib, near=(), kept=()):
    return pl.pallas_call(
        kernel,
        out_shape=[(pltpu.VMEM if n in kept else pltpu.HBM)(s, t) for n, (s, t) in enumerate(outs)],
        in_specs=[SMEM] * len(scalars) + [VMEM if n in near else HBM for n in range(len(arrays))],
        out_specs=[VMEM if n in kept else HBM for n in range(len(outs))],
        scratch_shapes=scratch,
        compiler_params=pltpu.CompilerParams(vmem_limit_bytes=vmem_mib << 20),
    )(*scalars, *arrays)


def start_call(tile, own, probe):
    shapes = [((2, HALF, 1024), F32), ((2, HALF, 1024), F32), ((2, HALF, WIN), F32)]
    return kernel_call(start_kernel, (tile,), (own, probe), shapes, [DMA((3,))], 2, kept=(0, 1, 2))


def table_call():
    quarter = pltpu.VMEM((WIN, WIN), BF16)
    tables = [stay(t) for t in dft_tables()]
    return kernel_call(table_kernel, (), tables, [(TABLE, BF16)] * 2, [quarter, quarter, DMA((2,))], 6, kept=(0, 1))


def forward_call(i, scalars, tables, fields, probes):
    return kernel_call(
        functools.partial(forward_kernel, i),
        scalars,
        (*tables, *fields, *probes),
        [((2, WIN, WIN), F32), ((4, WIN, 2 * WIN), F32), ((WIN, WIN), F32)],
        [pltpu.VMEM((2, 2 * WIN + 8, 512), F32), pltpu.VMEM((2, WIN, WIN), F32), DMA((4,))],
        14,
        near=(0, 1, *range(6, 12)),
        kept=(0, 1, 2),
    )


def backward_call(i, scalars, tables, mine, other, measured, patch, far, probes, prior):
    window, grad, half = (2, WIN + 8, 128), (4, 2, WIN, WIN), (4, 2, HALF, WIN)
    return kernel_call(
        functools.partial(backward_kernel, i),
        scalars,
        (*tables, mine, other, measured, patch, far, *probes, *prior),
        [(window, F32)] * 4 + ([(grad, F32)] if i == 0 else [(half, F32)] * 2),
        [
            pltpu.VMEM((2, WIN, WIN), F32),
            pltpu.VMEM((2, WIN + 8, 512), F32),
            pltpu.VMEM((2, WIN, WIN), F32),
            pltpu.VMEM((WIN, WIN), F32),
        ]
        + [DMA((2,))],
        16,
        near=(0, 1, 2, 3, 5, 6, *range(8, 15)),
        kept=range(6),
    )


def gather_call(scalars, pieces):
    shapes = [(2, WIN, 128), (2, WIN, 128), (2, 2, HALF, 128), (2, 2, HALF, 128)]
    scratch = [pltpu.VMEM((2, 2, 2 * WIN + 8, 128), F32)]
    return kernel_call(
        gather_kernel, scalars, pieces, [(s, F32) for s in shapes], scratch, 6, near=range(8), kept=range(4)
    )


def split_call(tile, keep, arrived):
    chunks = [((4, 2, 32, WIN), F32)] * 4
    return kernel_call(split_kernel, (tile,), (keep, arrived), chunks, [], 4, near=range(2), kept=range(4))


def stay(value):
    return pltpu.with_memory_space_constraint(value, pltpu.HBM)


def gradients(object_field, probe_modes, measured, row_starts, col_starts, live_counts):
    mode_index = lax.axis_index("mode").astype(jnp.int32)
    tile_index = lax.axis_index("tile").astype(jnp.int32)
    x, core = tile_index // 8, tile_index % 2
    mode, tile = mode_index.reshape(1), tile_index.reshape(1)
    scalars = (mode, tile, row_starts, col_starts)

    last, lead, part = start_call(tile, stay(object_field), stay(probe_modes))
    above = lax.ppermute(last, BOTH, TILE_UP)
    below = lax.ppermute(lead, BOTH, TILE_DOWN)
    near = [lax.ppermute(part, "mode", Y_PLUS[k]) for k in (1, 2, 3)]
    away = [lax.ppermute(near[k - 1], "tile", CORE_SWAP) for k in (1, 2, 3)]
    probes = [stay(probe_modes), *near, *away]
    tables = table_call()

    fields = (above, stay(object_field), below)
    fwd = [forward_call(i, scalars, tables, fields, probes) for i in range(2)]
    others = [lax.ppermute(fwd[i][2], "mode", Z_SWAP) for i in range(2)]

    pieces, prior = [], []
    for i in range(2):
        patch, far, mine = fwd[i]
        outs = backward_call(
            i, (*scalars, live_counts), tables, mine, others[i], stay(measured), patch, far, probes, prior
        )
        prior = [outs[4]]
        pieces += [outs[0]] + [lax.ppermute(outs[d], "mode", Y_PLUS[d]) for d in (1, 2, 3)]

    keep, give = outs[4], outs[5]
    arrived = lax.ppermute(give, "tile", CORE_SWAP)
    chunks = split_call(tile, keep, arrived)
    back = [lax.ppermute(chunks[k], "tile", X_XOR[k]) for k in (1, 2, 3)]
    total = (chunks[0] + back[0]) + (back[1] + back[2])
    back = [lax.ppermute(total[k], "mode", Y_PLUS[4 - k]) for k in (1, 2, 3)]
    total = (total[0] + back[0]) + (back[1] + back[2])
    back = [lax.ppermute(total, "tile", ZLO_XOR[k]) for k in (1, 2, 3)]
    total = (total + back[0]) + (back[1] + back[2])
    rows = [total] + [lax.ppermute(total, "tile", X_XOR[k]) for k in (1, 2, 3)]
    half = jnp.take(jnp.stack(rows, axis=1), jnp.arange(4) ^ x, axis=1).reshape(2, HALF, WIN)
    partner = lax.ppermute(half, "tile", CORE_SWAP)
    first = jnp.where(core == 0, half, partner)
    second = jnp.where(core == 0, partner, half)
    probe_grad = jnp.concatenate([first, second], axis=1)[:, None]

    mine, other, up, down = gather_call((mode, row_starts, col_starts), pieces)
    from_next = lax.ppermute(up, BOTH, TILE_DOWN)
    from_prev = lax.ppermute(down, BOTH, TILE_UP)
    z_hi = mode_index // 4

    def rims(which):
        above = lax.dynamic_index_in_dim(from_prev, which, 0, keepdims=False)
        below = lax.dynamic_index_in_dim(from_next, which, 0, keepdims=False)
        return jnp.concatenate([above, below], axis=1)

    crossed = lax.ppermute(other + rims(1 - z_hi), "mode", Z_SWAP)
    object_grad = (mine + rims(z_hi)) + crossed
    return (object_grad, probe_grad)


def solution(mesh):
    return jax.shard_map(
        gradients,
        mesh=mesh,
        in_specs=(
            P(None, "tile", None),
            P(None, "mode", None, None),
            P("tile", None, None),
            P("tile"),
            P("tile"),
            P("tile"),
        ),
        out_specs=(P(None, "tile", "mode"), P(None, "mode", None, None)),
        check_vma=False,
    )
```
